128 devices in a mesh: left: 8 (over z, core), right: 16 (over y, x).
Axes of the slice: x: 4, y: 4, z: 4, core: 2. Of those that a mesh axis runs over, the one named last changes fastest.
Arguments:
- wavefunction: bfloat16 [10240, 10240], P('left', 'right'), may hold values from -6 to 6
- left_env: bfloat16 [8, 10240, 640], P(None, 'left'), may hold values from -0.25 to 0.25
- right_env: bfloat16 [8, 640, 10240], P(None, None, 'right'), may hold values from -0.25 to 0.25
- left_sizes: int32 [16], replicated, may hold values from 512 to 640, as said below
- right_sizes: int32 [16], replicated, may hold values from 512 to 640, as said below
- allowed: int32 [31], replicated, may hold values 0 or 1
- channel_shift: int32 [8], replicated, may hold values from -1 to 1, as said below
Outputs:
- evolved: bfloat16 [10240, 10240], P('left', 'right')
The draws below stay inside these ranges and needn't reach their ends.
Inputs may be any that keep to these rules, and one draw needn't show every extreme that they name: `left_sizes`: multiples of 128; in every draw some left sector has exactly 640. `right_sizes`: multiples of 128; in every draw some right sector has exactly 640. `channel_shift`: each of -1, 0 and 1 occurs.
All inputs are finite; a program needn't handle non-finite values.
Results may differ from the reference program's by a relative error of at most 0.0054.
Values may be sent and summed in bfloat16 or wider, within the bound.
A program may use at most 192 MiB of HBM per device.

```python
import jax
import jax.numpy as jnp
from jax import lax

MAXS = 640
GRAIN = 128
CHANNELS = 8
STEPS = 2
LEFT_SECTORS = 16
RIGHT_SECTORS = 16
LEFT_ROWS = 10240
RIGHT_COLS = 10240


def draw_left_sizes(key, part):
    first_key, second_key = jax.random.split(key)
    grains = jax.random.randint(first_key, (LEFT_SECTORS,), MAXS // GRAIN - 1, MAXS // GRAIN + 1)
    widest = jax.random.randint(second_key, (), 0, LEFT_SECTORS)
    grains = jnp.where(jnp.arange(LEFT_SECTORS) == widest, MAXS // GRAIN, grains)
    return (grains * GRAIN).astype(jnp.int32)


def draw_right_sizes(key, part):
    first_key, second_key = jax.random.split(jax.random.fold_in(key, 7))
    grains = jax.random.randint(first_key, (RIGHT_SECTORS,), MAXS // GRAIN - 1, MAXS // GRAIN + 1)
    widest = jax.random.randint(second_key, (), 0, RIGHT_SECTORS)
    grains = jnp.where(jnp.arange(RIGHT_SECTORS) == widest, MAXS // GRAIN, grains)
    return (grains * GRAIN).astype(jnp.int32)


def draw_channel_shift(key, part):
    first_key, second_key = jax.random.split(jax.random.fold_in(key, 11))
    extra = jax.random.randint(first_key, (CHANNELS,), -1, 2)
    counter = jnp.arange(CHANNELS)
    base = jnp.where(counter < 3, counter - 1, extra)
    order = jax.random.permutation(second_key, CHANNELS)
    return base[order].astype(jnp.int32)


def set_ends(values, key, smallest, largest):
    index_at = [jax.random.randint(jax.random.fold_in(key, axis), (), 0, length) for axis, length in enumerate(values.shape)]
    widest = values.shape.index(max(values.shape))
    neighbour = index_at[:widest] + [(index_at[widest] + 1) % values.shape[widest]] + index_at[widest + 1:]
    return values.at[tuple(index_at)].set(smallest).at[tuple(neighbour)].set(largest)


def block_scale(rng, extent, cuts, least, largest):
    def one(position, blocks):
        steps = jax.random.uniform(jax.random.fold_in(jax.random.fold_in(rng, 6), position), (blocks,), jnp.float32, least / len(cuts), largest / len(cuts))
        return jnp.repeat(jnp.exp(steps), extent[position] // blocks).reshape((-1,) + (1,) * (len(extent) - position - 1))

    gain = one(*cuts[0])
    for cut in cuts[1:]:
        gain = gain * one(*cut)
    return gain


def scatter_about(rng, shape, scale, bound, cuts=(), kind=jnp.bfloat16):
    result = jax.random.normal(rng, shape, jnp.float32) * scale
    if len(cuts) > 0:
        result = block_scale(rng, shape, cuts, -0.22, 0.18) * result
    return jnp.clip(result, min=-bound, max=bound).astype(kind)


def setup_inputs(seed: int = 0) -> dict:
    keys = jax.random.split(jax.random.key(seed), 8)
    wavefunction = scatter_about(keys[0], (LEFT_ROWS, RIGHT_COLS), 1.0, 6.0, ((0, 8), (1, 16)))
    left_env = scatter_about(keys[1], (CHANNELS, LEFT_ROWS, MAXS), MAXS ** -0.5, 0.25, ((1, 8),))
    right_env = scatter_about(keys[2], (CHANNELS, MAXS, RIGHT_COLS), MAXS ** -0.5, 0.25, ((2, 16),))
    left_sizes = draw_left_sizes(jax.random.fold_in(keys[7], 71), 0)
    right_sizes = draw_right_sizes(jax.random.fold_in(keys[7], 71), 0)
    allowed = set_ends((jax.random.randint(keys[5], (LEFT_SECTORS + RIGHT_SECTORS - 1,), 0, 3) < 2).astype(jnp.int32), jax.random.fold_in(keys[5], 1), 0, 1)
    channel_shift = draw_channel_shift(jax.random.fold_in(keys[7], 71), 0)
    return {"wavefunction": wavefunction, "left_env": left_env, "right_env": right_env, "left_sizes": left_sizes, "right_sizes": right_sizes, "allowed": allowed, "channel_shift": channel_shift}


time_step = 0.5


def keep_factor(left_sizes, right_sizes, allowed):
    positions = jnp.arange(MAXS, dtype=jnp.int32)
    row_keep = (positions[None, :] < left_sizes[:, None]).astype(jnp.float32)
    col_keep = (positions[None, :] < right_sizes[:, None]).astype(jnp.float32)
    sector_left = jnp.arange(LEFT_SECTORS, dtype=jnp.int32)
    sector_right = jnp.arange(RIGHT_SECTORS, dtype=jnp.int32)
    blocks = allowed[sector_left[:, None] + sector_right[None, :]].astype(jnp.float32)
    return row_keep[:, :, None, None] * blocks[:, None, :, None] * col_keep[None, None, :, :]


def masked(values, factor):
    shaped = values.reshape(LEFT_SECTORS, MAXS, RIGHT_SECTORS, MAXS)
    return (shaped * factor).reshape(LEFT_ROWS, RIGHT_COLS)


def reference(wavefunction, left_env, right_env, left_sizes, right_sizes, allowed, channel_shift):
    factor = keep_factor(left_sizes, right_sizes, allowed)
    current = masked(wavefunction.astype(jnp.float32), factor).astype(jnp.bfloat16)
    for taylor_step in range(STEPS):
        slots = current.reshape(LEFT_SECTORS, MAXS, RIGHT_COLS)
        empty_rows = jnp.zeros((1, MAXS, RIGHT_COLS), jnp.bfloat16)
        padded = jnp.concatenate([empty_rows, slots, empty_rows], axis=0)
        applied = jnp.zeros((LEFT_ROWS, RIGHT_COLS), jnp.float32)
        for channel in range(CHANNELS):
            shift_now = channel_shift[channel]
            sources = lax.dynamic_slice_in_dim(padded, (1 - shift_now).astype(jnp.int32), LEFT_SECTORS, 0)
            blocks = left_env[channel].reshape(LEFT_SECTORS, MAXS, MAXS)
            partial_value = jnp.einsum("sik,skc->sic", blocks.astype(jnp.float32), sources.astype(jnp.float32))
            partial_value = partial_value.astype(jnp.bfloat16).reshape(LEFT_ROWS, RIGHT_SECTORS, MAXS)
            empty_cols = jnp.zeros((LEFT_ROWS, 1, MAXS), jnp.bfloat16)
            widened = jnp.concatenate([empty_cols, partial_value, empty_cols], axis=1)
            picked = lax.dynamic_slice_in_dim(widened, (1 + shift_now).astype(jnp.int32), RIGHT_SECTORS, 1)
            right_blocks = right_env[channel].reshape(MAXS, RIGHT_SECTORS, MAXS)
            term = jnp.einsum("rjk,kjc->rjc", picked.astype(jnp.float32), right_blocks.astype(jnp.float32))
            applied = applied + term.reshape(LEFT_ROWS, RIGHT_COLS)
        current = masked(current.astype(jnp.float32) - time_step * applied, factor).astype(jnp.bfloat16)
    return current
```

```python
import jax
import jax.numpy as jnp
from jax import lax
from jax.experimental import pallas as pl
from jax.experimental.pallas import tpu as pltpu
from jax.sharding import PartitionSpec as P

MAXS = 640
STEPS = 2
CHUNK = 256
ROW_TILE = 320
COMPUTE = True

time_step = 0.5

CHUNKS = tuple((at, min(CHUNK, MAXS - at)) for at in range(0, MAXS, CHUNK))
PARTS = len(CHUNKS)
MESH = pl.DeviceIdType.MESH


def kernel(left_sizes, right_sizes, allowed, channel_shift, wave, left_env, right_env, out, *scratch):
    scratch = list(scratch)
    lbuf, acc, half = scratch[:3]
    rbuf = scratch[3 : 3 + PARTS]
    flat = scratch[3 + PARTS : 3 + PARTS + 4 * PARTS]
    wave_sem, left_sem, right_sem, send_sem, recv_sem = scratch[3 + 5 * PARTS :]
    xs = [[flat[(2 * t + b) * PARTS : (2 * t + b + 1) * PARTS] for b in range(2)] for t in range(2)]
    channels = lbuf.shape[1]
    rows, cols = lax.axis_size("left"), lax.axis_size("right")
    me, col = lax.axis_index("left"), lax.axis_index("right")
    up, down = lax.rem(me + rows - 1, rows), lax.rem(me + 1, rows)
    before, after = lax.rem(col + cols - 1, cols), lax.rem(col + 1, cols)

    def fetch_wave(b, c):
        at, width = CHUNKS[c]
        return pltpu.make_async_copy(
            wave.at[pl.ds(b * MAXS, MAXS), pl.ds(at, width)], xs[0][b][c].at[1], wave_sem.at[b, c]
        )

    def fetch_left(b):
        return pltpu.make_async_copy(left_env.at[:, pl.ds(b * MAXS, MAXS), :], lbuf.at[b], left_sem.at[b])

    def fetch_right(c):
        at, width = CHUNKS[c]
        return pltpu.make_async_copy(right_env.at[:, pl.ds(at, width), :], rbuf[c], right_sem.at[c])

    for b in (1, 0):
        for c in range(PARTS):
            fetch_wave(b, c).start()
    fetch_left(0).start()
    for c in range(PARTS):
        fetch_right(c).start()
    fetch_left(1).start()

    barrier = pltpu.get_barrier_semaphore()
    for peer in ((me, before), (up, after), (down, before), (me, after)):
        pl.semaphore_signal(barrier, inc=1, device_id=peer, device_id_type=MESH)
    pl.semaphore_wait(barrier, 4)

    def copies(t, b, c):
        targets = ((2, (me if b == 0 else down, before)), (0, (up if b == 0 else me, after)))
        return [
            pltpu.make_async_remote_copy(
                src_ref=xs[t][b][c].at[1],
                dst_ref=xs[t][1 - b][c].at[slot],
                send_sem=send_sem.at[t, b, c, side],
                recv_sem=recv_sem.at[t, 1 - b, c, side],
                device_id=target,
                device_id_type=MESH,
            )
            for side, (slot, target) in enumerate(targets)
        ]

    def push(t, b, c):
        for copy in copies(t, b, c):
            copy.start()

    def arrive(t, b, c):
        for copy in copies(t, 1 - b, c):
            copy.wait_recv()
        no_after = col == cols - 1
        no_before = col == 0
        if b == 0:
            no_after = no_after | (me == 0)
        else:
            no_before = no_before | (me == rows - 1)
        for slot, missing in ((2, no_after), (0, no_before)):

            @pl.when(missing)
            def _():
                xs[t][b][c][slot] = jnp.zeros(xs[t][b][c].shape[1:], jnp.bfloat16)

    def keep(b, c):
        at, width = CHUNKS[c]
        sector = 2 * me + b
        row = lax.broadcasted_iota(jnp.int32, (MAXS, width), 0)
        column = lax.broadcasted_iota(jnp.int32, (MAXS, width), 1) + at
        row_limit = jnp.where(allowed[sector + col] == 1, left_sizes[sector], 0)
        return (row < row_limit) & (column < right_sizes[col])

    def absorb(t, b, c):
        width = CHUNKS[c][1]

        def channel(w, carry):
            source = xs[t][b][c][channel_shift[w] + 1]
            product = jnp.dot(lbuf[b, w], source, preferred_element_type=jnp.float32)
            half[:, pl.ds(pl.multiple_of(w * width, width), width)] = product.astype(jnp.bfloat16)
            return carry

        lax.fori_loop(0, channels, channel, 0)

        def tile(m, carry):
            span = pl.ds(pl.multiple_of(m * ROW_TILE, ROW_TILE), ROW_TILE)
            part = jnp.dot(
                half[span, : channels * width],
                rbuf[c][...].reshape(channels * width, MAXS),
                preferred_element_type=jnp.float32,
            )
            if c == 0:
                acc[span, :] = part
            else:
                acc[span, :] += part
            return carry

        lax.fori_loop(0, MAXS // ROW_TILE, tile, 0)

    def finish(t, b):
        for c, (at, width) in enumerate(CHUNKS):
            value = xs[t][b][c][1].astype(jnp.float32) - time_step * acc[:, at : at + width]
            value = jnp.where(keep(b, c), value, 0.0).astype(jnp.bfloat16)
            if t == 0:
                xs[1][b][c][1] = value
            else:
                out[b * MAXS : (b + 1) * MAXS, at : at + width] = value

    for b in (1, 0):
        for c in range(PARTS):
            fetch_wave(b, c).wait()
            value = xs[0][b][c][1].astype(jnp.float32)
            xs[0][b][c][1] = jnp.where(keep(b, c), value, 0.0).astype(jnp.bfloat16)
            if b == 1:
                push(0, 1, c)

    for t, b, follow in ((0, 0, (0, 0)), (0, 1, (1, 0)), (1, 1, (1, 1)), (1, 0, None)):
        if t == 0:
            fetch_left(b).wait()
        for c in range(PARTS):
            arrive(t, b, c)
            if follow is not None:
                push(*follow, c)
            if t == 0 and b == 0:
                fetch_right(c).wait()
            if COMPUTE:
                absorb(t, b, c)
        finish(t, b)

    for t in range(2):
        for b in range(2):
            for c in range(PARTS):
                for copy in copies(t, b, c):
                    copy.wait_send()


def body(wavefunction, left_env, right_env, left_sizes, right_sizes, allowed, channel_shift):
    channels = left_env.shape[0]
    scalars = pl.BlockSpec(memory_space=pltpu.SMEM)
    anywhere = pl.BlockSpec(memory_space=pl.ANY)
    return pl.pallas_call(
        kernel,
        out_shape=jax.ShapeDtypeStruct(wavefunction.shape, jnp.bfloat16),
        in_specs=[scalars] * 4 + [anywhere] * 3,
        out_specs=pl.BlockSpec(memory_space=pltpu.VMEM),
        scratch_shapes=[
            pltpu.VMEM((2, channels, MAXS, MAXS), jnp.bfloat16),
            pltpu.VMEM((MAXS, MAXS), jnp.float32),
            pltpu.VMEM((MAXS, channels * CHUNK), jnp.bfloat16),
            *[pltpu.VMEM((channels, width, MAXS), jnp.bfloat16) for _, width in CHUNKS],
            *[pltpu.VMEM((3, MAXS, width), jnp.bfloat16) for _ in range(4) for _, width in CHUNKS],
            pltpu.SemaphoreType.DMA((2, PARTS)),
            pltpu.SemaphoreType.DMA((2,)),
            pltpu.SemaphoreType.DMA((PARTS,)),
            pltpu.SemaphoreType.DMA((2, 2, PARTS, 2)),
            pltpu.SemaphoreType.DMA((2, 2, PARTS, 2)),
        ],
        compiler_params=pltpu.CompilerParams(
            collective_id=0, has_side_effects=True, vmem_limit_bytes=56 * 2**20
        ),
        name="taylor",
    )(left_sizes, right_sizes, allowed, channel_shift, wavefunction, left_env, right_env)


def solution(mesh):
    return jax.shard_map(
        body,
        mesh=mesh,
        in_specs=(P("left", "right"), P(None, "left", None), P(None, None, "right"), P(), P(), P(), P()),
        out_specs=P("left", "right"),
        check_vma=False,
    )
```

```python
import jax
import jax.numpy as jnp
from jax import lax
from jax.experimental import pallas as pl
from jax.experimental.pallas import tpu as pltpu
from jax.sharding import PartitionSpec as P

MAXS = 640
STEPS = 2
CHUNK = 128
UNROLL = 4

time_step = 0.5

CHUNKS = tuple((at, min(CHUNK, MAXS - at)) for at in range(0, MAXS, CHUNK))
PARTS = len(CHUNKS)
MESH = pl.DeviceIdType.MESH


def kernel(left_sizes_in, right_sizes_in, allowed_in, channel_shift_in, wave, left_env, right_env, out, *scratch):
    scratch = list(scratch)
    lbuf, acc, half = scratch[:3]
    rbuf = scratch[3 : 3 + PARTS]
    flat = scratch[3 + PARTS : 3 + PARTS + 4 * PARTS]
    left_sizes, right_sizes, allowed, channel_shift = scratch[3 + 5 * PARTS : 7 + 5 * PARTS]
    wave_sem, left_sem, right_sem, send_sem, recv_sem, small_sem = scratch[7 + 5 * PARTS :]
    xs = [[flat[(2 * t + b) * PARTS : (2 * t + b + 1) * PARTS] for b in range(2)] for t in range(2)]
    channels = lbuf.shape[1]
    rows, cols = lax.axis_size("left"), lax.axis_size("right")
    me, col = lax.axis_index("left"), lax.axis_index("right")
    up, down = lax.rem(me + rows - 1, rows), lax.rem(me + 1, rows)
    before, after = lax.rem(col + cols - 1, cols), lax.rem(col + 1, cols)

    def fetch_wave(b, c):
        at, width = CHUNKS[c]
        return pltpu.make_async_copy(
            wave.at[pl.ds(b * MAXS, MAXS), pl.ds(at, width)], xs[0][b][c].at[1], wave_sem.at[b, c]
        )

    def fetch_left(b):
        return pltpu.make_async_copy(left_env.at[:, pl.ds(b * MAXS, MAXS), :], lbuf.at[b], left_sem.at[b])

    def fetch_right(c):
        at, width = CHUNKS[c]
        return pltpu.make_async_copy(right_env.at[:, pl.ds(at, width), :], rbuf[c], right_sem.at[c])

    small = [
        pltpu.make_async_copy(source, target, small_sem.at[i])
        for i, (source, target) in enumerate(
            (
                (left_sizes_in, left_sizes),
                (right_sizes_in, right_sizes),
                (allowed_in, allowed),
                (channel_shift_in, channel_shift),
            )
        )
    ]
    for copy in small:
        copy.start()
    for b in (1, 0):
        for c in range(PARTS):
            fetch_wave(b, c).start()
    fetch_left(0).start()
    for c in range(PARTS):
        fetch_right(c).start()
    fetch_left(1).start()

    barrier = pltpu.get_barrier_semaphore()
    for peer in ((me, before), (up, after), (down, before), (me, after)):
        pl.semaphore_signal(barrier, inc=1, device_id=peer, device_id_type=MESH)
    pl.semaphore_wait(barrier, 4)

    def copies(t, b, c):
        targets = ((2, (me if b == 0 else down, before)), (0, (up if b == 0 else me, after)))
        return [
            pltpu.make_async_remote_copy(
                src_ref=xs[t][b][c].at[1],
                dst_ref=xs[t][1 - b][c].at[slot],
                send_sem=send_sem.at[t, b, c, side],
                recv_sem=recv_sem.at[t, 1 - b, c, side],
                device_id=target,
                device_id_type=MESH,
            )
            for side, (slot, target) in enumerate(targets)
        ]

    def push(t, b, c):
        for copy in copies(t, b, c):
            copy.start()

    def arrive(t, b, c):
        for copy in copies(t, 1 - b, c):
            copy.wait_recv()
        no_after = col == cols - 1
        no_before = col == 0
        if b == 0:
            no_after = no_after | (me == 0)
        else:
            no_before = no_before | (me == rows - 1)
        for slot, missing in ((2, no_after), (0, no_before)):

            @pl.when(missing)
            def _():
                xs[t][b][c][slot] = jnp.zeros(xs[t][b][c].shape[1:], jnp.bfloat16)

    def keep(b, c):
        at, width = CHUNKS[c]
        sector = 2 * me + b
        row = lax.broadcasted_iota(jnp.int32, (MAXS, width), 0)
        column = lax.broadcasted_iota(jnp.int32, (MAXS, width), 1) + at
        row_limit = jnp.where(allowed[sector + col] == 1, left_sizes[sector], 0)
        return (row < row_limit) & (column < right_sizes[col])

    def absorb(t, b, c):
        width = CHUNKS[c][1]

        def channel(w, carry):
            source = xs[t][b][c][channel_shift[w] + 1]
            product = jnp.dot(lbuf[b, w], source, preferred_element_type=jnp.float32)
            half[:, pl.ds(pl.multiple_of(w * width, width), width)] = product.astype(jnp.bfloat16)
            return carry

        lax.fori_loop(0, channels, channel, 0, unroll=UNROLL)
        total = jnp.dot(
            half[:, : channels * width],
            rbuf[c][...].reshape(channels * width, MAXS),
            preferred_element_type=jnp.float32,
        )
        if c > 0:
            total += acc[...]
        if c < PARTS - 1:
            acc[...] = total
            return
        for part, (at, width) in enumerate(CHUNKS):
            value = xs[t][b][part][1].astype(jnp.float32) - time_step * total[:, at : at + width]
            value = jnp.where(keep(b, part), value, 0.0).astype(jnp.bfloat16)
            if t == 0:
                xs[1][b][part][1] = value
            else:
                out[b * MAXS : (b + 1) * MAXS, at : at + width] = value

    for copy in small:
        copy.wait()
    for b in (1, 0):
        for c in range(PARTS):
            fetch_wave(b, c).wait()
            value = xs[0][b][c][1].astype(jnp.float32)
            xs[0][b][c][1] = jnp.where(keep(b, c), value, 0.0).astype(jnp.bfloat16)
            if b == 1:
                push(0, 1, c)

    for t, b, follow in ((0, 0, (0, 0)), (0, 1, (1, 0)), (1, 1, (1, 1)), (1, 0, None)):
        if t == 0:
            fetch_left(b).wait()
        for c in range(PARTS):
            arrive(t, b, c)
            if follow is not None:
                push(*follow, c)
            if t == 0 and b == 0:
                fetch_right(c).wait()
            absorb(t, b, c)

    for t in range(2):
        for b in range(2):
            for c in range(PARTS):
                for copy in copies(t, b, c):
                    copy.wait_send()


def body(wavefunction, left_env, right_env, left_sizes, right_sizes, allowed, channel_shift):
    channels = left_env.shape[0]
    anywhere = pl.BlockSpec(memory_space=pl.ANY)
    return pl.pallas_call(
        kernel,
        out_shape=jax.ShapeDtypeStruct(wavefunction.shape, jnp.bfloat16),
        in_specs=[anywhere] * 7,
        out_specs=pl.BlockSpec(memory_space=pltpu.VMEM),
        scratch_shapes=[
            pltpu.VMEM((2, channels, MAXS, MAXS), jnp.bfloat16),
            pltpu.VMEM((MAXS, MAXS), jnp.float32),
            pltpu.VMEM((MAXS, channels * CHUNK), jnp.bfloat16),
            *[pltpu.VMEM((channels, width, MAXS), jnp.bfloat16) for _, width in CHUNKS],
            *[pltpu.VMEM((3, MAXS, width), jnp.bfloat16) for _ in range(4) for _, width in CHUNKS],
            *[pltpu.SMEM(v.shape, v.dtype) for v in (left_sizes, right_sizes, allowed, channel_shift)],
            pltpu.SemaphoreType.DMA((2, PARTS)),
            pltpu.SemaphoreType.DMA((2,)),
            pltpu.SemaphoreType.DMA((PARTS,)),
            pltpu.SemaphoreType.DMA((2, 2, PARTS, 2)),
            pltpu.SemaphoreType.DMA((2, 2, PARTS, 2)),
            pltpu.SemaphoreType.DMA((4,)),
        ],
        compiler_params=pltpu.CompilerParams(
            collective_id=0, has_side_effects=True, vmem_limit_bytes=52 * 2**20
        ),
        name="taylor",
    )(
        *[
            pltpu.with_memory_space_constraint(v, pltpu.HBM)
            for v in (left_sizes, right_sizes, allowed, channel_shift, wavefunction, left_env, right_env)
        ]
    )


def solution(mesh):
    return jax.shard_map(
        body,
        mesh=mesh,
        in_specs=(P("left", "right"), P(None, "left", None), P(None, None, "right"), P(), P(), P(), P()),
        out_specs=P("left", "right"),
        check_vma=False,
    )
```

```python
import jax
import jax.numpy as jnp
from jax import lax
from jax.experimental import pallas as pl
from jax.experimental.pallas import tpu as pltpu
from jax.sharding import PartitionSpec as P

MAXS = 640
STEPS = 2
WIDTH = 128
PARTS = MAXS // WIDTH
SPLIT = 384
UNROLL = 8

time_step = 0.5

MESH = pl.DeviceIdType.MESH


def kernel(
    left_sizes_in,
    right_sizes_in,
    allowed_in,
    channel_shift_in,
    wave,
    left_env,
    right_env,
    out,
    lbuf,
    rbuf,
    acc,
    half,
    early,
    stage,
    x00,
    x01,
    x10,
    x11,
    left_sizes,
    right_sizes,
    allowed,
    channel_shift,
    small_sem,
    wave_sem,
    left_sem,
    right_sem,
    send_sem,
    recv_sem,
):
    xs = ((x00, x01), (x10, x11))
    channels = lbuf.shape[1]
    rows, cols = lax.axis_size("left"), lax.axis_size("right")
    me, col = lax.axis_index("left"), lax.axis_index("right")
    up, down = lax.rem(me + rows - 1, rows), lax.rem(me + 1, rows)
    before, after = lax.rem(col + cols - 1, cols), lax.rem(col + 1, cols)

    def columns(c):
        return pl.ds(c * WIDTH if isinstance(c, int) else pl.multiple_of(c * WIDTH, WIDTH), WIDTH)

    def fetch_wave(b, c):
        return pltpu.make_async_copy(
            wave.at[pl.ds(b * MAXS, MAXS), columns(c)], xs[0][b].at[c, 1], wave_sem.at[b, c]
        )

    def fetch_left(b):
        return pltpu.make_async_copy(left_env.at[:, pl.ds(b * MAXS, MAXS), :], lbuf.at[b], left_sem.at[b])

    def fetch_right(c):
        return pltpu.make_async_copy(right_env.at[:, columns(c), :], rbuf.at[c], right_sem.at[c])

    small = [
        pltpu.make_async_copy(source, target, small_sem.at[i])
        for i, (source, target) in enumerate(
            (
                (left_sizes_in, left_sizes),
                (right_sizes_in, right_sizes),
                (allowed_in, allowed),
                (channel_shift_in, channel_shift),
            )
        )
    ]
    for copy in small:
        copy.start()
    for b in (1, 0):
        for c in range(PARTS):
            fetch_wave(b, c).start()
    fetch_left(0).start()
    for c in range(PARTS):
        fetch_right(c).start()
    fetch_left(1).start()

    barrier = pltpu.get_barrier_semaphore()
    for peer in ((me, before), (up, after), (down, before), (me, after)):
        pl.semaphore_signal(barrier, inc=1, device_id=peer, device_id_type=MESH)
    pl.semaphore_wait(barrier, 4)

    def pieces(t, b, c):
        if t == STEPS - 1 and b == 1 and isinstance(c, int) and c == PARTS - 1:
            return ((c, 0, SPLIT), (PARTS, SPLIT, MAXS - SPLIT))
        return ((c, 0, MAXS),)

    def copies(t, b, c, piece):
        index, first, count = piece
        targets = ((2, (me if b == 0 else down, before)), (0, (up if b == 0 else me, after)))
        return [
            pltpu.make_async_remote_copy(
                src_ref=xs[t][b].at[c, 1, pl.ds(first, count)],
                dst_ref=xs[t][1 - b].at[c, slot, pl.ds(first, count)],
                send_sem=send_sem.at[t, b, index, side],
                recv_sem=recv_sem.at[t, 1 - b, index, side],
                device_id=target,
                device_id_type=MESH,
            )
            for side, (slot, target) in enumerate(targets)
        ]

    def push(t, b, c):
        for piece in pieces(t, b, c):
            for copy in copies(t, b, c, piece):
                copy.start()

    def arrive(t, b, c, piece):
        for copy in copies(t, 1 - b, c, piece):
            copy.wait_recv()

    def put(t, b, c, piece):
        span = pl.ds(piece[1], piece[2])
        for slot in range(3):
            stage[slot, span, :] = xs[t][b][c, slot, span, :]
        no_after, no_before = col == cols - 1, col == 0
        if b == 0:
            no_after = no_after | (me == 0)
        else:
            no_before = no_before | (me == rows - 1)
        for slot, missing in ((2, no_after), (0, no_before)):

            @pl.when(missing)
            def _():
                stage[slot, span, :] = jnp.zeros((piece[2], WIDTH), jnp.bfloat16)

    def keep(b, c):
        sector = 2 * me + b
        row = lax.broadcasted_iota(jnp.int32, (MAXS, WIDTH), 0)
        column = lax.broadcasted_iota(jnp.int32, (MAXS, WIDTH), 1) + c * WIDTH
        row_limit = jnp.where(allowed[sector + col] == 1, left_sizes[sector], 0)
        return (row < row_limit) & (column < right_sizes[col])

    def each_channel(step):
        lax.fori_loop(0, channels, step, 0, unroll=UNROLL)

    def first_product(b):
        def channel(w, carry):
            product = jnp.dot(lbuf[b, w], stage[channel_shift[w] + 1], preferred_element_type=jnp.float32)
            half[:, columns(w)] = product.astype(jnp.bfloat16)
            return carry

        each_channel(channel)

    def second_product(c):
        return jnp.dot(
            half[...], rbuf[c].reshape(channels * WIDTH, MAXS), preferred_element_type=jnp.float32
        )

    def finish(t, b, total):
        for c in range(PARTS):
            value = xs[t][b][c, 1].astype(jnp.float32) - time_step * total[:, c * WIDTH : (c + 1) * WIDTH]
            value = jnp.where(keep(b, c), value, 0.0).astype(jnp.bfloat16)
            if t == 0:
                xs[1][b][c, 1] = value
            else:
                out[b * MAXS : (b + 1) * MAXS, c * WIDTH : (c + 1) * WIDTH] = value

    for copy in small:
        copy.wait()
    for b in (1, 0):

        def begin(c, carry):
            fetch_wave(b, c).wait()
            value = xs[0][b][c, 1].astype(jnp.float32)
            xs[0][b][c, 1] = jnp.where(keep(b, c), value, 0.0).astype(jnp.bfloat16)
            if b == 1:
                push(0, 1, c)
            return carry

        lax.fori_loop(0, PARTS, begin, 0)

    for t, b, follow in ((0, 0, (0, 0)), (0, 1, (1, 0)), (1, 1, (1, 1)), (1, 0, None)):
        if t == 0:
            fetch_left(b).wait()

        def take(c, piece):
            arrive(t, b, c, piece)
            if follow is not None and piece[0] is c:
                push(*follow, c)
            if t == 0 and b == 0:
                fetch_right(c).wait()
            put(t, b, c, piece)

        acc[...] = jnp.zeros(acc.shape, jnp.float32)

        def absorb(c, carry):
            take(c, (c, 0, MAXS))
            first_product(b)
            acc[...] += second_product(c)
            return carry

        lax.fori_loop(0, PARTS - 1, absorb, 0)
        last = PARTS - 1
        if (t, b) != (STEPS - 1, 0):
            take(last, (last, 0, MAXS))
            first_product(b)
        else:
            top, rest = pieces(t, 1 - b, last)
            take(last, top)

            def early_channel(w, carry):
                early[:, columns(w)] = jnp.dot(
                    lbuf[b, w, :, :SPLIT],
                    stage[channel_shift[w] + 1, :SPLIT],
                    preferred_element_type=jnp.float32,
                )
                return carry

            each_channel(early_channel)
            take(last, rest)

            def late_channel(w, carry):
                product = jnp.dot(
                    lbuf[b, w, :, SPLIT:],
                    stage[channel_shift[w] + 1, SPLIT:],
                    preferred_element_type=jnp.float32,
                )
                half[:, columns(w)] = (early[:, columns(w)] + product).astype(jnp.bfloat16)
                return carry

            each_channel(late_channel)
        finish(t, b, acc[...] + second_product(last))

    for t in range(STEPS):
        for b in range(2):
            for c in range(PARTS):
                for piece in pieces(t, b, c):
                    for copy in copies(t, b, c, piece):
                        copy.wait_send()


def body(wavefunction, left_env, right_env, left_sizes, right_sizes, allowed, channel_shift):
    channels = left_env.shape[0]
    arguments = (left_sizes, right_sizes, allowed, channel_shift, wavefunction, left_env, right_env)
    return pl.pallas_call(
        kernel,
        out_shape=jax.ShapeDtypeStruct(wavefunction.shape, jnp.bfloat16),
        in_specs=[pl.BlockSpec(memory_space=pl.ANY)] * len(arguments),
        out_specs=pl.BlockSpec(memory_space=pltpu.VMEM),
        scratch_shapes=[
            pltpu.VMEM((2, channels, MAXS, MAXS), jnp.bfloat16),
            pltpu.VMEM((PARTS, channels, WIDTH, MAXS), jnp.bfloat16),
            pltpu.VMEM((MAXS, MAXS), jnp.float32),
            pltpu.VMEM((MAXS, channels * WIDTH), jnp.bfloat16),
            pltpu.VMEM((MAXS, channels * WIDTH), jnp.float32),
            pltpu.VMEM((3, MAXS, WIDTH), jnp.bfloat16),
            *[pltpu.VMEM((PARTS, 3, MAXS, WIDTH), jnp.bfloat16)] * 4,
            *[pltpu.SMEM(v.shape, v.dtype) for v in arguments[:4]],
            pltpu.SemaphoreType.DMA((4,)),
            pltpu.SemaphoreType.DMA((2, PARTS)),
            pltpu.SemaphoreType.DMA((2,)),
            pltpu.SemaphoreType.DMA((PARTS,)),
            pltpu.SemaphoreType.DMA((STEPS, 2, PARTS + 1, 2)),
            pltpu.SemaphoreType.DMA((STEPS, 2, PARTS + 1, 2)),
        ],
        compiler_params=pltpu.CompilerParams(
            collective_id=0, has_side_effects=True, vmem_limit_bytes=52 * 2**20
        ),
        name="taylor",
    )(*[pltpu.with_memory_space_constraint(v, pltpu.HBM) for v in arguments])


def solution(mesh):
    return jax.shard_map(
        body,
        mesh=mesh,
        in_specs=(P("left", "right"), P(None, "left", None), P(None, None, "right"), P(), P(), P(), P()),
        out_specs=P("left", "right"),
        check_vma=False,
    )
```

```python
import jax
import jax.numpy as jnp
from jax import lax
from jax.experimental import pallas as pl
from jax.experimental.pallas import tpu as pltpu
from jax.sharding import PartitionSpec as P

MAXS = 640
STEPS = 2
WIDTH = 128
PARTS = MAXS // WIDTH
SPLIT = 384
UNROLL = 8
WINDOW = 3

time_step = 0.5

MESH = pl.DeviceIdType.MESH


def kernel(
    left_sizes_in,
    right_sizes_in,
    allowed_in,
    channel_shift_in,
    wave,
    left_env,
    right_env,
    out,
    lbuf,
    rbuf,
    acc,
    half,
    early,
    stage,
    relay,
    x00,
    x01,
    x10,
    x11,
    left_sizes,
    right_sizes,
    allowed,
    channel_shift,
    small_sem,
    wave_sem,
    left_sem,
    right_sem,
    send_sem,
    recv_sem,
    hop_send_sem,
    hop_recv_sem,
    pass_sem,
):
    xs = ((x00, x01), (x10, x11))
    channels = lbuf.shape[1]
    rows, cols = lax.axis_size("left"), lax.axis_size("right")
    me, col = lax.axis_index("left"), lax.axis_index("right")
    up, down = lax.rem(me + rows - 1, rows), lax.rem(me + 1, rows)
    before, after = lax.rem(col + cols - 1, cols), lax.rem(col + 1, cols)

    def columns(c):
        return pl.ds(c * WIDTH if isinstance(c, int) else pl.multiple_of(c * WIDTH, WIDTH), WIDTH)

    def fetch_wave(b, c):
        return pltpu.make_async_copy(
            wave.at[pl.ds(b * MAXS, MAXS), columns(c)], xs[0][b].at[c, 1], wave_sem.at[b, c]
        )

    def fetch_left(b):
        return pltpu.make_async_copy(left_env.at[:, pl.ds(b * MAXS, MAXS), :], lbuf.at[b], left_sem.at[b])

    def fetch_right(c):
        return pltpu.make_async_copy(right_env.at[:, columns(c), :], rbuf.at[c], right_sem.at[c])

    small = [
        pltpu.make_async_copy(source, target, small_sem.at[i])
        for i, (source, target) in enumerate(
            (
                (left_sizes_in, left_sizes),
                (right_sizes_in, right_sizes),
                (allowed_in, allowed),
                (channel_shift_in, channel_shift),
            )
        )
    ]
    for copy in small:
        copy.start()
    for b in (1, 0):
        for c in range(PARTS):
            fetch_wave(b, c).start()
    fetch_left(0).start()
    for c in range(PARTS):
        fetch_right(c).start()
    fetch_left(1).start()

    barrier = pltpu.get_barrier_semaphore()
    has_up, has_down, has_before, has_after = me > 0, me < rows - 1, col > 0, col < cols - 1
    even = lax.rem(me, 2) == 0
    peers = (
        (has_before, (me, before)),
        (has_after, (me, after)),
        (has_up & has_after, (up, after)),
        (has_down & has_before, (down, before)),
        (has_up & even, (up, col)),
        (has_down & jnp.logical_not(even), (down, col)),
    )
    for present, peer in peers:

        @pl.when(present)
        def _():
            pl.semaphore_signal(barrier, inc=1, device_id=peer, device_id_type=MESH)

    pl.semaphore_wait(barrier, sum(present.astype(jnp.int32) for present, _ in peers))

    def pieces(t, b, c):
        if t == STEPS - 1 and b == 1 and isinstance(c, int) and c == PARTS - 1:
            return ((c, 0, SPLIT), (PARTS, SPLIT, MAXS - SPLIT))
        return ((c, 0, MAXS),)

    def relayed(b, c, sender):
        found = jnp.bool_(False)
        for z in range(1, rows // 2):
            count = round((rows // 2 - z) * PARTS / (rows // 2))
            found = found | ((sender == (2 * z if b == 0 else rows - 1 - 2 * z)) & (c >= PARTS - count))
        return found & (has_after if b == 0 else has_before)

    def hop(t, b, c):
        return pltpu.make_async_remote_copy(
            src_ref=xs[t][b].at[c, 1],
            dst_ref=relay.at[t, b, c],
            send_sem=hop_send_sem.at[t, b, c],
            recv_sem=hop_recv_sem.at[t, b, c],
            device_id=(up if b == 0 else down, col),
            device_id_type=MESH,
        )

    def copy_of(t, b, c, piece, side, passing=False):
        index, first, count = piece
        along = (me, before if side == 0 else after)
        diagonal = (down, before) if b == 1 else (up, after)
        source = relay.at[t, b, c] if passing else xs[t][b].at[c, 1]
        return pltpu.make_async_remote_copy(
            src_ref=source.at[pl.ds(first, count)],
            dst_ref=xs[t][1 - b].at[c, 2 if side == 0 else 0, pl.ds(first, count)],
            send_sem=pass_sem.at[t, b, index] if passing else send_sem.at[t, b, index, side],
            recv_sem=recv_sem.at[t, 1 - b, index, side],
            device_id=along if side == b or passing else diagonal,
            device_id_type=MESH,
        )

    straight = (has_before, has_after)
    across = (has_up & has_after, has_down & has_before)

    def own(t, b, c, act):
        for piece in pieces(t, b, c):

            @pl.when(straight[b])
            def _():
                act(copy_of(t, b, c, piece, b))

            @pl.when(across[b] & jnp.logical_not(relayed(b, c, me)))
            def _():
                act(copy_of(t, b, c, piece, 1 - b))

    def passed(t, b, c, act, arrived=None):
        @pl.when(relayed(b, c, me + 1 if b == 0 else me - 1))
        def _():
            if arrived is not None:
                arrived(hop(t, b, c))
            for piece in pieces(t, b, c):
                act(copy_of(t, b, c, piece, 1 - b, passing=True))

    def begin_hop(t, b, c):
        @pl.when(relayed(b, c, me))
        def _():
            hop(t, b, c).start()

    def start(copy):
        copy.start()

    def sent(copy):
        copy.wait_send()

    def landed(copy):
        copy.wait_recv()

    def push(t, b, c):
        own(t, b, c, start)
        passed(t, b, c, start, landed)

    def arrive(t, b, c, piece):
        @pl.when(has_after if b == 1 else has_before)
        def _():
            copy_of(t, 1 - b, c, piece, 1 - b).wait_recv()

        @pl.when(has_up & has_after if b == 0 else has_down & has_before)
        def _():
            copy_of(t, 1 - b, c, piece, b).wait_recv()

    def put(t, b, c, piece):
        span = pl.ds(piece[1], piece[2])
        for slot in range(3):
            stage[slot, span, :] = xs[t][b][c, slot, span, :]
        no_after = jnp.logical_not(has_up & has_after if b == 0 else has_after)
        no_before = jnp.logical_not(has_before if b == 0 else has_down & has_before)
        for slot, missing in ((2, no_after), (0, no_before)):

            @pl.when(missing)
            def _():
                stage[slot, span, :] = jnp.zeros((piece[2], WIDTH), jnp.bfloat16)

    def keep(b, c):
        sector = 2 * me + b
        row = lax.broadcasted_iota(jnp.int32, (MAXS, WIDTH), 0)
        column = lax.broadcasted_iota(jnp.int32, (MAXS, WIDTH), 1) + c * WIDTH
        row_limit = jnp.where(allowed[sector + col] == 1, left_sizes[sector], 0)
        return (row < row_limit) & (column < right_sizes[col])

    def each_channel(step):
        lax.fori_loop(0, channels, step, 0, unroll=UNROLL)

    def first_product(b):
        def channel(w, carry):
            product = jnp.dot(lbuf[b, w], stage[channel_shift[w] + 1], preferred_element_type=jnp.float32)
            half[:, columns(w)] = product.astype(jnp.bfloat16)
            return carry

        each_channel(channel)

    def second_product(c):
        return jnp.dot(
            half[...], rbuf[c].reshape(channels * WIDTH, MAXS), preferred_element_type=jnp.float32
        )

    def finish(t, b, total):
        for c in range(PARTS):
            value = xs[t][b][c, 1].astype(jnp.float32) - time_step * total[:, c * WIDTH : (c + 1) * WIDTH]
            value = jnp.where(keep(b, c), value, 0.0).astype(jnp.bfloat16)
            if t == 0:
                xs[1][b][c, 1] = value
            else:
                out[b * MAXS : (b + 1) * MAXS, c * WIDTH : (c + 1) * WIDTH] = value

    for copy in small:
        copy.wait()
    for b in (1, 0):

        def begin(c, carry):
            fetch_wave(b, c).wait()
            value = xs[0][b][c, 1].astype(jnp.float32)
            xs[0][b][c, 1] = jnp.where(keep(b, c), value, 0.0).astype(jnp.bfloat16)
            begin_hop(0, b, c)
            if b == 1:

                @pl.when(c < WINDOW)
                def _():
                    own(0, 1, c, start)

            return carry

        lax.fori_loop(0, PARTS, begin, 0)

    def begin_passing(c, carry):
        passed(0, 1, c, start, landed)
        return carry

    lax.fori_loop(0, WINDOW, begin_passing, 0)

    order = ((0, 1), (0, 0), (1, 0), (1, 1))

    def advance(phase, c):
        later = c + WINDOW
        if isinstance(c, int):
            if phase + 1 < len(order):
                push(*order[phase + 1], later - PARTS)
            return

        if phase + 1 < len(order):

            @pl.when(later >= PARTS)
            def _():
                push(*order[phase + 1], later - PARTS)

        @pl.when(later < PARTS - 1)
        def _():
            push(*order[phase], later)

        @pl.when(later == PARTS - 1)
        def _():
            push(*order[phase], PARTS - 1)

    for phase, (t, b) in enumerate(((0, 0), (0, 1), (1, 1), (1, 0))):
        if t == 0:
            fetch_left(b).wait()

        def take(c, piece):
            arrive(t, b, c, piece)
            if piece[0] is c:
                advance(phase, c)
            if t == 0 and b == 0:
                fetch_right(c).wait()
            put(t, b, c, piece)

        acc[...] = jnp.zeros(acc.shape, jnp.float32)

        def absorb(c, carry):
            take(c, (c, 0, MAXS))
            first_product(b)
            acc[...] += second_product(c)
            return carry

        lax.fori_loop(0, PARTS - 1, absorb, 0)
        last = PARTS - 1
        if (t, b) != (STEPS - 1, 0):
            take(last, (last, 0, MAXS))
            first_product(b)
        else:
            top, rest = pieces(t, 1 - b, last)
            take(last, top)

            def early_channel(w, carry):
                early[:, columns(w)] = jnp.dot(
                    lbuf[b, w, :, :SPLIT],
                    stage[channel_shift[w] + 1, :SPLIT],
                    preferred_element_type=jnp.float32,
                )
                return carry

            each_channel(early_channel)
            take(last, rest)

            def late_channel(w, carry):
                product = jnp.dot(
                    lbuf[b, w, :, SPLIT:],
                    stage[channel_shift[w] + 1, SPLIT:],
                    preferred_element_type=jnp.float32,
                )
                half[:, columns(w)] = (early[:, columns(w)] + product).astype(jnp.bfloat16)
                return carry

            each_channel(late_channel)
        finish(t, b, acc[...] + second_product(last))
        if t == 0:

            def next_hop(c, carry):
                begin_hop(1, b, c)
                return carry

            lax.fori_loop(0, PARTS, next_hop, 0)

    for t in range(STEPS):
        for b in range(2):

            def end(c, carry):
                own(t, b, c, sent)
                passed(t, b, c, sent)

                @pl.when(relayed(b, c, me))
                def _():
                    hop(t, b, c).wait_send()

                return carry

            lax.fori_loop(0, PARTS - 1, end, 0)
            end(PARTS - 1, 0)


def body(wavefunction, left_env, right_env, left_sizes, right_sizes, allowed, channel_shift):
    channels = left_env.shape[0]
    arguments = (left_sizes, right_sizes, allowed, channel_shift, wavefunction, left_env, right_env)
    return pl.pallas_call(
        kernel,
        out_shape=jax.ShapeDtypeStruct(wavefunction.shape, jnp.bfloat16),
        in_specs=[pl.BlockSpec(memory_space=pl.ANY)] * len(arguments),
        out_specs=pl.BlockSpec(memory_space=pltpu.VMEM),
        scratch_shapes=[
            pltpu.VMEM((2, channels, MAXS, MAXS), jnp.bfloat16),
            pltpu.VMEM((PARTS, channels, WIDTH, MAXS), jnp.bfloat16),
            pltpu.VMEM((MAXS, MAXS), jnp.float32),
            pltpu.VMEM((MAXS, channels * WIDTH), jnp.bfloat16),
            pltpu.VMEM((MAXS, channels * WIDTH), jnp.float32),
            pltpu.VMEM((3, MAXS, WIDTH), jnp.bfloat16),
            pltpu.VMEM((STEPS, 2, PARTS, MAXS, WIDTH), jnp.bfloat16),
            *[pltpu.VMEM((PARTS, 3, MAXS, WIDTH), jnp.bfloat16)] * 4,
            *[pltpu.SMEM(v.shape, v.dtype) for v in arguments[:4]],
            pltpu.SemaphoreType.DMA((4,)),
            pltpu.SemaphoreType.DMA((2, PARTS)),
            pltpu.SemaphoreType.DMA((2,)),
            pltpu.SemaphoreType.DMA((PARTS,)),
            pltpu.SemaphoreType.DMA((STEPS, 2, PARTS + 1, 2)),
            pltpu.SemaphoreType.DMA((STEPS, 2, PARTS + 1, 2)),
            pltpu.SemaphoreType.DMA((STEPS, 2, PARTS)),
            pltpu.SemaphoreType.DMA((STEPS, 2, PARTS)),
            pltpu.SemaphoreType.DMA((STEPS, 2, PARTS + 1)),
        ],
        compiler_params=pltpu.CompilerParams(
            collective_id=0, has_side_effects=True, vmem_limit_bytes=52 * 2**20
        ),
        name="taylor",
    )(*[pltpu.with_memory_space_constraint(v, pltpu.HBM) for v in arguments])


def solution(mesh):
    return jax.shard_map(
        body,
        mesh=mesh,
        in_specs=(P("left", "right"), P(None, "left", None), P(None, None, "right"), P(), P(), P(), P()),
        out_specs=P("left", "right"),
        check_vma=False,
    )
```

```python
import jax
import jax.numpy as jnp
from jax import lax
from jax.experimental import pallas as pl
from jax.experimental.pallas import tpu as pltpu
from jax.sharding import PartitionSpec as P

MAXS = 640
STEPS = 2
WIDTH = 128
PARTS = MAXS // WIDTH
SPLIT = 384
UNROLL = 8
WINDOW = 3

time_step = 0.5

MESH = pl.DeviceIdType.MESH


def kernel(
    left_sizes_in,
    right_sizes_in,
    allowed_in,
    channel_shift_in,
    wave,
    left_env,
    right_env,
    out,
    lbuf,
    rbuf,
    acc,
    half,
    early,
    stage,
    relay,
    x00,
    x01,
    x10,
    x11,
    left_sizes,
    right_sizes,
    allowed,
    channel_shift,
    small_sem,
    wave_sem,
    left_sem,
    right_sem,
    send_sem,
    recv_sem,
    hop_send_sem,
    hop_recv_sem,
    pass_sem,
):
    xs = ((x00, x01), (x10, x11))
    channels = lbuf.shape[1]
    rows, cols = lax.axis_size("left"), lax.axis_size("right")
    me, col = lax.axis_index("left"), lax.axis_index("right")
    up, down = lax.rem(me + rows - 1, rows), lax.rem(me + 1, rows)
    before, after = lax.rem(col + cols - 1, cols), lax.rem(col + 1, cols)

    def columns(c):
        return pl.ds(c * WIDTH if isinstance(c, int) else pl.multiple_of(c * WIDTH, WIDTH), WIDTH)

    def fetch_wave(b, c):
        return pltpu.make_async_copy(
            wave.at[pl.ds(b * MAXS, MAXS), columns(c)], xs[0][b].at[c, 1], wave_sem.at[b, c]
        )

    def fetch_left(b):
        return pltpu.make_async_copy(left_env.at[:, pl.ds(b * MAXS, MAXS), :], lbuf.at[b], left_sem.at[b])

    def fetch_right(c):
        return pltpu.make_async_copy(right_env.at[:, columns(c), :], rbuf.at[c], right_sem.at[c])

    small = [
        pltpu.make_async_copy(source, target, small_sem.at[i])
        for i, (source, target) in enumerate(
            (
                (left_sizes_in, left_sizes),
                (right_sizes_in, right_sizes),
                (allowed_in, allowed),
                (channel_shift_in, channel_shift),
            )
        )
    ]
    for copy in small:
        copy.start()
    for b in (1, 0):
        for c in range(PARTS):
            fetch_wave(b, c).start()
    fetch_left(0).start()
    for c in range(PARTS):
        fetch_right(c).start()
    fetch_left(1).start()

    barrier = pltpu.get_barrier_semaphore()
    has_up, has_down, has_before, has_after = me > 0, me < rows - 1, col > 0, col < cols - 1
    even = lax.rem(me, 2) == 0
    peers = (
        (has_before, (me, before)),
        (has_after, (me, after)),
        (has_up & has_after, (up, after)),
        (has_down & has_before, (down, before)),
        (has_up & even, (up, col)),
        (has_down & jnp.logical_not(even), (down, col)),
    )
    for present, peer in peers:

        @pl.when(present)
        def _():
            pl.semaphore_signal(barrier, inc=1, device_id=peer, device_id_type=MESH)

    pl.semaphore_wait(barrier, sum(present.astype(jnp.int32) for present, _ in peers))

    def pieces(t, b, c):
        if t == STEPS - 1 and b == 1 and isinstance(c, int) and c == PARTS - 1:
            return ((c, 0, SPLIT), (PARTS, SPLIT, MAXS - SPLIT))
        return ((c, 0, MAXS),)

    def relayed(b, c, sender):
        found = jnp.bool_(False)
        for z in range(1, rows // 2):
            count = round((rows // 2 - z) * PARTS / (rows // 2))
            found = found | ((sender == (2 * z if b == 0 else rows - 1 - 2 * z)) & (c >= PARTS - count))
        return found & (has_after if b == 0 else has_before)

    def hop(t, b, c):
        return pltpu.make_async_remote_copy(
            src_ref=xs[t][b].at[c, 1],
            dst_ref=relay.at[t, b, c],
            send_sem=hop_send_sem.at[t, b, c],
            recv_sem=hop_recv_sem.at[t, b, c],
            device_id=(up if b == 0 else down, col),
            device_id_type=MESH,
        )

    def copy_of(t, b, c, piece, side, passing=False):
        index, first, count = piece
        along = (me, before if side == 0 else after)
        diagonal = (down, before) if b == 1 else (up, after)
        source = relay.at[t, b, c] if passing else xs[t][b].at[c, 1]
        return pltpu.make_async_remote_copy(
            src_ref=source.at[pl.ds(first, count)],
            dst_ref=xs[t][1 - b].at[c, 2 if side == 0 else 0, pl.ds(first, count)],
            send_sem=pass_sem.at[t, b, index] if passing else send_sem.at[t, b, index, side],
            recv_sem=recv_sem.at[t, 1 - b, index, side],
            device_id=along if side == b or passing else diagonal,
            device_id_type=MESH,
        )

    straight = (has_before, has_after)
    across = (has_up & has_after, has_down & has_before)

    def own(t, b, c, act):
        for piece in pieces(t, b, c):

            @pl.when(straight[b])
            def _():
                act(copy_of(t, b, c, piece, b))

            @pl.when(across[b] & jnp.logical_not(relayed(b, c, me)))
            def _():
                act(copy_of(t, b, c, piece, 1 - b))

    def passed(t, b, c, act, arrived=None):
        @pl.when(relayed(b, c, me + 1 if b == 0 else me - 1))
        def _():
            if arrived is not None:
                arrived(hop(t, b, c))
            for piece in pieces(t, b, c):
                act(copy_of(t, b, c, piece, 1 - b, passing=True))

    def begin_hop(t, b, c):
        @pl.when(relayed(b, c, me))
        def _():
            hop(t, b, c).start()

    def start(copy):
        copy.start()

    def sent(copy):
        copy.wait_send()

    def landed(copy):
        copy.wait_recv()

    def push(t, b, c):
        passed(t, b, c, start, landed)
        own(t, b, c, start)

    def arrive(t, b, c, piece):
        @pl.when(has_after if b == 1 else has_before)
        def _():
            copy_of(t, 1 - b, c, piece, 1 - b).wait_recv()

        @pl.when(has_up & has_after if b == 0 else has_down & has_before)
        def _():
            copy_of(t, 1 - b, c, piece, b).wait_recv()

    def put(t, b, c, piece):
        span = pl.ds(piece[1], piece[2])
        for slot in range(3):
            stage[slot, span, :] = xs[t][b][c, slot, span, :]
        no_after = jnp.logical_not(has_up & has_after if b == 0 else has_after)
        no_before = jnp.logical_not(has_before if b == 0 else has_down & has_before)
        for slot, missing in ((2, no_after), (0, no_before)):

            @pl.when(missing)
            def _():
                stage[slot, span, :] = jnp.zeros((piece[2], WIDTH), jnp.bfloat16)

    def keep(b, c):
        sector = 2 * me + b
        row = lax.broadcasted_iota(jnp.int32, (MAXS, WIDTH), 0)
        column = lax.broadcasted_iota(jnp.int32, (MAXS, WIDTH), 1) + c * WIDTH
        row_limit = jnp.where(allowed[sector + col] == 1, left_sizes[sector], 0)
        return (row < row_limit) & (column < right_sizes[col])

    def each_channel(step):
        lax.fori_loop(0, channels, step, 0, unroll=UNROLL)

    def first_product(b):
        def channel(w, carry):
            product = jnp.dot(lbuf[b, w], stage[channel_shift[w] + 1], preferred_element_type=jnp.float32)
            half[:, columns(w)] = product.astype(jnp.bfloat16)
            return carry

        each_channel(channel)

    def second_product(c):
        return jnp.dot(
            half[...], rbuf[c].reshape(channels * WIDTH, MAXS), preferred_element_type=jnp.float32
        )

    def finish(t, b, total):
        for c in range(PARTS):
            value = xs[t][b][c, 1].astype(jnp.float32) - time_step * total[:, c * WIDTH : (c + 1) * WIDTH]
            value = jnp.where(keep(b, c), value, 0.0).astype(jnp.bfloat16)
            if t == 0:
                xs[1][b][c, 1] = value
            else:
                out[b * MAXS : (b + 1) * MAXS, c * WIDTH : (c + 1) * WIDTH] = value

    for copy in small:
        copy.wait()
    for b in (1, 0):

        def begin(c, carry):
            fetch_wave(b, c).wait()
            value = xs[0][b][c, 1].astype(jnp.float32)
            xs[0][b][c, 1] = jnp.where(keep(b, c), value, 0.0).astype(jnp.bfloat16)
            begin_hop(0, b, c)
            if b == 1:

                @pl.when(c < WINDOW)
                def _():
                    own(0, 1, c, start)

            return carry

        lax.fori_loop(0, PARTS, begin, 0)

    def begin_passing(c, carry):
        passed(0, 1, c, start, landed)
        return carry

    lax.fori_loop(0, WINDOW, begin_passing, 0)

    order = ((0, 1), (0, 0), (1, 0), (1, 1))

    def advance(phase, c):
        later = c + WINDOW
        if isinstance(c, int):
            if phase + 1 < len(order):
                push(*order[phase + 1], later - PARTS)
            return

        if phase + 1 < len(order):

            @pl.when(later >= PARTS)
            def _():
                push(*order[phase + 1], later - PARTS)

        @pl.when(later < PARTS - 1)
        def _():
            push(*order[phase], later)

        @pl.when(later == PARTS - 1)
        def _():
            push(*order[phase], PARTS - 1)

    for phase, (t, b) in enumerate(((0, 0), (0, 1), (1, 1), (1, 0))):
        if t == 0:
            fetch_left(b).wait()

        def take(c, piece):
            arrive(t, b, c, piece)
            if piece[0] is c:
                advance(phase, c)
            if t == 0 and b == 0:
                fetch_right(c).wait()
            put(t, b, c, piece)

        acc[...] = jnp.zeros(acc.shape, jnp.float32)

        def absorb(c, carry):
            take(c, (c, 0, MAXS))
            first_product(b)
            acc[...] += second_product(c)
            return carry

        lax.fori_loop(0, PARTS - 1, absorb, 0)
        last = PARTS - 1
        if (t, b) != (STEPS - 1, 0):
            take(last, (last, 0, MAXS))
            first_product(b)
        else:
            top, rest = pieces(t, 1 - b, last)
            take(last, top)

            def early_channel(w, carry):
                early[:, columns(w)] = jnp.dot(
                    lbuf[b, w, :, :SPLIT],
                    stage[channel_shift[w] + 1, :SPLIT],
                    preferred_element_type=jnp.float32,
                )
                return carry

            each_channel(early_channel)
            take(last, rest)

            def late_channel(w, carry):
                product = jnp.dot(
                    lbuf[b, w, :, SPLIT:],
                    stage[channel_shift[w] + 1, SPLIT:],
                    preferred_element_type=jnp.float32,
                )
                half[:, columns(w)] = (early[:, columns(w)] + product).astype(jnp.bfloat16)
                return carry

            each_channel(late_channel)
        finish(t, b, acc[...] + second_product(last))
        if t == 0:

            def next_hop(c, carry):
                begin_hop(1, b, c)
                return carry

            lax.fori_loop(0, PARTS, next_hop, 0)

    for t in range(STEPS):
        for b in range(2):

            def end(c, carry):
                own(t, b, c, sent)
                passed(t, b, c, sent)

                @pl.when(relayed(b, c, me))
                def _():
                    hop(t, b, c).wait_send()

                return carry

            lax.fori_loop(0, PARTS - 1, end, 0)
            end(PARTS - 1, 0)


def body(wavefunction, left_env, right_env, left_sizes, right_sizes, allowed, channel_shift):
    channels = left_env.shape[0]
    arguments = (left_sizes, right_sizes, allowed, channel_shift, wavefunction, left_env, right_env)
    return pl.pallas_call(
        kernel,
        out_shape=jax.ShapeDtypeStruct(wavefunction.shape, jnp.bfloat16),
        in_specs=[pl.BlockSpec(memory_space=pl.ANY)] * len(arguments),
        out_specs=pl.BlockSpec(memory_space=pltpu.VMEM),
        scratch_shapes=[
            pltpu.VMEM((2, channels, MAXS, MAXS), jnp.bfloat16),
            pltpu.VMEM((PARTS, channels, WIDTH, MAXS), jnp.bfloat16),
            pltpu.VMEM((MAXS, MAXS), jnp.float32),
            pltpu.VMEM((MAXS, channels * WIDTH), jnp.bfloat16),
            pltpu.VMEM((MAXS, channels * WIDTH), jnp.float32),
            pltpu.VMEM((3, MAXS, WIDTH), jnp.bfloat16),
            pltpu.VMEM((STEPS, 2, PARTS, MAXS, WIDTH), jnp.bfloat16),
            *[pltpu.VMEM((PARTS, 3, MAXS, WIDTH), jnp.bfloat16)] * 4,
            *[pltpu.SMEM(v.shape, v.dtype) for v in arguments[:4]],
            pltpu.SemaphoreType.DMA((4,)),
            pltpu.SemaphoreType.DMA((2, PARTS)),
            pltpu.SemaphoreType.DMA((2,)),
            pltpu.SemaphoreType.DMA((PARTS,)),
            pltpu.SemaphoreType.DMA((STEPS, 2, PARTS + 1, 2)),
            pltpu.SemaphoreType.DMA((STEPS, 2, PARTS + 1, 2)),
            pltpu.SemaphoreType.DMA((STEPS, 2, PARTS)),
            pltpu.SemaphoreType.DMA((STEPS, 2, PARTS)),
            pltpu.SemaphoreType.DMA((STEPS, 2, PARTS + 1)),
        ],
        compiler_params=pltpu.CompilerParams(
            collective_id=0, has_side_effects=True, vmem_limit_bytes=52 * 2**20
        ),
        name="taylor",
    )(*[pltpu.with_memory_space_constraint(v, pltpu.HBM) for v in arguments])


def solution(mesh):
    return jax.shard_map(
        body,
        mesh=mesh,
        in_specs=(P("left", "right"), P(None, "left", None), P(None, None, "right"), P(), P(), P(), P()),
        out_specs=P("left", "right"),
        check_vma=False,
    )
```
